32 devices in a mesh: groups: 2 (over y), seq: 4 (over z), mp: 4 (over x, core).
Axes of the slice: x: 2, y: 2, z: 4, core: 2. Of those that a mesh axis runs over, the one named last changes fastest.
Arguments:
- nucleotide_features: bfloat16 [3072, 1536], P(('groups', 'seq')), parts along dimension 0, may hold values from -36 to 36
- location_table: bfloat16 [1536, 1536], P('seq'), may hold values from -6 to 6
- premix_rescaler: float32 [1536], replicated, may hold values from 0.5 to 1.5
- probe_lookup_matrices: bfloat16 [2, 1536, 1024], P(None, None, 'mp'), may hold values from -0.15625 to 0.15625
- payload_projector: bfloat16 [1536, 1536], P(None, 'mp'), may hold values from -0.15625 to 0.15625
- logit_sharpness: float32 [8], P('mp'), may hold values from 8 to 32
- mixing_projector: bfloat16 [1536, 1536], P('mp'), may hold values from -0.15625 to 0.15625
- premlp_rescaler: float32 [1536], replicated, may hold values from 0.5 to 1.5
- widening_matrix: bfloat16 [1536, 3072], P(None, 'mp'), may hold values from -0.15625 to 0.15625
- narrowing_matrix: bfloat16 [3072, 1536], P('mp'), may hold values from -0.109375 to 0.109375
Outputs:
- averaged: float32 [3072, 1536], P(('groups', 'seq'), 'mp'), parts along dimension 0
The draws below stay inside these ranges and needn't reach their ends.
There are 2 independent parts, one for each index of `groups`. The reference program is written for one: setup_inputs(seed, part) draws one part's arguments, and reference() takes and returns one part's arrays. A program takes and returns all parts, laid end to end along the dimension named above; an argument that names none is the same for every part. Nothing has to cross between parts.
All inputs are finite; a program needn't handle non-finite values.
Results may differ from the reference program's by a relative error of at most 0.0033.
Values may be sent and summed in bfloat16 or wider, within the bound.
A program may use at most 128 MiB of HBM per device.

```python
import math
import jax
import jax.numpy as jnp
from jax import lax

D = 1536
NUM_SUBSPACES = 8
QK = 128
VD = 192
FF = 3072
SEQ_LEN = 1536


def draw_nucleotide_features(key, part):
    key_rows, key_cols, key_base = jax.random.split(key, 3)
    row_scale = jnp.exp(jax.random.uniform(key_rows, (SEQ_LEN, 1), jnp.float32, math.log(0.3), math.log(3.0)))
    col_scale = jnp.exp(jax.random.uniform(key_cols, (1, D), jnp.float32, math.log(0.3), math.log(3.0)))
    payload_vectors = jnp.clip(jax.random.normal(key_base, (SEQ_LEN, D), jnp.float32), -4.0, 4.0)
    return (payload_vectors * row_scale * col_scale).astype(jnp.bfloat16)


def levels(key, dims, pieces, low, largest):
    gain, own = 1.0, jax.random.fold_in(key, 6)
    for dim, blocks in pieces:
        heights = jnp.exp(jax.random.uniform(jax.random.fold_in(own, dim), (blocks,), jnp.float32, low / len(pieces), largest / len(pieces)))
        gain = gain * jnp.repeat(heights, dims[dim] // blocks).reshape([-1 if axis == dim else 1 for axis in range(len(dims))])
    return gain


def gaussian(rng, extent, spread, most, cuts=(), kind=jnp.bfloat16):
    level = levels(rng, extent, cuts, -0.22, 0.18) if cuts else 1.0
    result = jax.random.normal(rng, extent, jnp.float32) * spread * level
    return jnp.minimum(jnp.maximum(result, -most), most).astype(kind)


def setup_inputs(seed: int = 0, part: int = 0) -> dict:
    arg_keys = jax.random.split(jax.random.key(seed), 11)
    part_keys = jax.random.split(jax.random.fold_in(arg_keys[10], part), 11)
    nucleotide_features = draw_nucleotide_features(jax.random.fold_in(jax.random.fold_in(arg_keys[10], part), 71), part)
    location_table = gaussian(arg_keys[1], (SEQ_LEN, D), 1.0, 6.0, ((0, 4),))
    premix_rescaler = jnp.clip(1.0 + 0.1 * jax.random.normal(arg_keys[2], (D,), jnp.float32), 0.5, 1.5)
    probe_lookup_matrices = gaussian(arg_keys[3], (2, D, NUM_SUBSPACES * QK), D ** -0.5, 0.15625, ((2, 4),))
    payload_projector = gaussian(arg_keys[4], (D, NUM_SUBSPACES * VD), D ** -0.5, 0.15625, ((1, 4),))
    logit_sharpness = jnp.clip(jnp.exp(math.log(32.0) - 1.3862944 * jax.random.uniform(arg_keys[5], (NUM_SUBSPACES,), jnp.float32) ** levels(arg_keys[5], (NUM_SUBSPACES,), ((0, 4),), -0.2, 0.2)), 8.0, 32.0)
    mixing_projector = gaussian(arg_keys[6], (NUM_SUBSPACES * VD, D), (NUM_SUBSPACES * VD) ** -0.5, 0.15625, ((0, 4),))
    premlp_rescaler = jnp.clip(1.0 + 0.1 * jax.random.normal(arg_keys[7], (D,), jnp.float32), 0.5, 1.5)
    widening_matrix = gaussian(arg_keys[8], (D, FF), D ** -0.5, 0.15625, ((1, 4),))
    narrowing_matrix = gaussian(arg_keys[9], (FF, D), FF ** -0.5, 0.109375, ((0, 4),))
    return {"nucleotide_features": nucleotide_features, "location_table": location_table, "premix_rescaler": premix_rescaler, "probe_lookup_matrices": probe_lookup_matrices, "payload_projector": payload_projector, "logit_sharpness": logit_sharpness, "mixing_projector": mixing_projector, "premlp_rescaler": premlp_rescaler, "widening_matrix": widening_matrix, "narrowing_matrix": narrowing_matrix}


epsilon = 1e-06

def normalize(payload_vectors):
    return payload_vectors * lax.rsqrt(lax.optimization_barrier(jnp.mean(payload_vectors * payload_vectors, axis=-1, keepdims=True)) + epsilon)

def twin_helix_transformer(running_sum_hidden, premix_rescaler, probe_lookup_matrices, payload_projector, logit_sharpness, mixing_projector, premlp_rescaler, widening_matrix, narrowing_matrix):
    length = running_sum_hidden.shape[0]
    subspace_results = logit_sharpness.shape[0]
    lookup_dimension = probe_lookup_matrices.shape[2] // subspace_results
    value_size = payload_projector.shape[1] // subspace_results
    normed = (normalize(running_sum_hidden) * premix_rescaler).astype(jnp.bfloat16)
    query = jnp.dot(normed, probe_lookup_matrices[0], preferred_element_type=jnp.float32).reshape(length, subspace_results, lookup_dimension)
    keys = jnp.dot(normed, probe_lookup_matrices[1], preferred_element_type=jnp.float32).reshape(length, subspace_results, lookup_dimension)
    probe_unit_vectors = normalize(query).astype(jnp.bfloat16)
    lookup_unit_vectors = normalize(keys).astype(jnp.bfloat16)
    payload_vectors = jnp.dot(normed, payload_projector, preferred_element_type=jnp.float32).astype(jnp.bfloat16).reshape(length, subspace_results, value_size)

    def one_subspace(inputs):
        query_head, key_head, value_head, scale_head = inputs
        scores = jnp.dot(query_head, key_head.T, preferred_element_type=jnp.float32) * (scale_head / lookup_dimension)
        weight_exp = jnp.exp(scores)
        totals = lax.optimization_barrier(jnp.sum(weight_exp, axis=1, keepdims=True))
        numer = jnp.dot(weight_exp.astype(jnp.bfloat16), value_head, preferred_element_type=jnp.float32)
        return (numer / totals).astype(jnp.bfloat16)
    mixed_positions = lax.map(one_subspace, (jnp.transpose(probe_unit_vectors, (1, 0, 2)), jnp.transpose(lookup_unit_vectors, (1, 0, 2)), jnp.transpose(payload_vectors, (1, 0, 2)), logit_sharpness))
    mixed_positions = jnp.transpose(mixed_positions, (1, 0, 2)).reshape(length, subspace_results * value_size)
    middle = running_sum_hidden + jnp.dot(mixed_positions, mixing_projector, preferred_element_type=jnp.float32)
    normed_mid = (normalize(middle) * premlp_rescaler).astype(jnp.bfloat16)
    expanded = jax.nn.gelu(jnp.dot(normed_mid, widening_matrix, preferred_element_type=jnp.float32), approximate=True).astype(jnp.bfloat16)
    return middle + jnp.dot(expanded, narrowing_matrix, preferred_element_type=jnp.float32)

def reference(nucleotide_features, location_table, premix_rescaler, probe_lookup_matrices, payload_projector, logit_sharpness, mixing_projector, premlp_rescaler, widening_matrix, narrowing_matrix):
    reversed_tokens = jnp.flip(nucleotide_features, 0)
    plus_sequence = nucleotide_features.astype(jnp.float32) + location_table.astype(jnp.float32)
    complement_sequence = reversed_tokens.astype(jnp.float32) + location_table.astype(jnp.float32)
    plus_result = twin_helix_transformer(plus_sequence, premix_rescaler, probe_lookup_matrices, payload_projector, logit_sharpness, mixing_projector, premlp_rescaler, widening_matrix, narrowing_matrix)
    complement_result = twin_helix_transformer(complement_sequence, premix_rescaler, probe_lookup_matrices, payload_projector, logit_sharpness, mixing_projector, premlp_rescaler, widening_matrix, narrowing_matrix)
    return 0.5 * (plus_result + jnp.flip(complement_result, 0))
```

```python
import functools

import jax
import jax.numpy as jnp
from jax import lax
from jax.experimental import pallas as pl
from jax.experimental.pallas import tpu as pltpu
from jax.sharding import PartitionSpec as P

epsilon = 1e-06
MESH = pl.DeviceIdType.MESH
f32 = jnp.float32
bf16 = jnp.bfloat16


def normalize(v):
    return v * lax.rsqrt(jnp.mean(v * v, axis=-1, keepdims=True) + epsilon)


def gather_kernel(nz, nm, *refs):
    src = refs[0:2]
    out = refs[2:4]
    stage, lsem, zs, zr, xs, xr, cs, cr = refs[4:]
    nx = nm // 2
    z = lax.axis_index("seq")
    m = lax.axis_index("mp")
    x, c = m // 2, m % 2
    rows = src[0].shape[0]
    piece = rows // nm

    def at(zsrc, mm):
        return pl.ds(pl.multiple_of(zsrc * rows + mm * piece, piece), piece)

    others = [lax.rem(x + d, nx) for d in range(1, nx)]
    barrier = pltpu.get_barrier_semaphore()

    @pl.when(z > 0)
    def _():
        pl.semaphore_signal(barrier, inc=1, device_id={"seq": z - 1}, device_id_type=MESH)

    @pl.when(z < nz - 1)
    def _():
        pl.semaphore_signal(barrier, inc=1, device_id={"seq": z + 1}, device_id_type=MESH)

    for o in others:
        pl.semaphore_signal(barrier, inc=1, device_id={"mp": o * 2 + c}, device_id_type=MESH)
    pl.semaphore_signal(barrier, inc=1, device_id={"mp": x * 2 + 1 - c}, device_id_type=MESH)

    loads = [pltpu.make_async_copy(src[a], stage.at[a], lsem.at[a]) for a in range(2)]
    for cp in loads:
        cp.start()

    pl.semaphore_wait(barrier, nx + jnp.where(z > 0, 1, 0) + jnp.where(z < nz - 1, 1, 0))

    def zsend(a, dist, right):
        zsrc = z - dist if right else z + dist
        s = at(zsrc, m)
        if dist == 0:
            ref = src[a].at[pl.ds(pl.multiple_of(m * piece, piece), piece)]
        else:
            ref = out[a].at[s]
        k = 0 if right else 1
        return pltpu.make_async_remote_copy(
            src_ref=ref, dst_ref=out[a].at[s],
            send_sem=zs.at[a, k, dist], recv_sem=zr.at[a, k, dist],
            device_id={"seq": z + 1 if right else z - 1}, device_id_type=MESH)

    def zrecv(a, dist, right):
        zsrc = z - dist if right else z + dist
        s = at(zsrc, m)
        k = 0 if right else 1
        return pltpu.make_async_remote_copy(
            src_ref=out[a].at[s], dst_ref=out[a].at[s],
            send_sem=zs.at[a, k, dist - 1], recv_sem=zr.at[a, k, dist - 1],
            device_id={"seq": z + 1 if right else z - 1}, device_id_type=MESH)

    def xcopy(a, k, dist, d, right, mine):
        zsrc = z - dist if right else z + dist
        o = lax.rem(x + d, nx) if mine else lax.rem(x - d + nx, nx)
        s = at(zsrc, m if mine else o * 2 + c)
        return pltpu.make_async_remote_copy(
            src_ref=out[a].at[s], dst_ref=out[a].at[s],
            send_sem=xs.at[a, k, dist - 1, d - 1], recv_sem=xr.at[a, k, dist - 1, d - 1],
            device_id={"mp": o * 2 + c}, device_id_type=MESH)

    def ccopy(a, k, dist, d, right, mine):
        zsrc = z - dist if right else z + dist
        o = lax.rem(x - d + nx, nx)
        s = at(zsrc, o * 2 + (c if mine else 1 - c))
        return pltpu.make_async_remote_copy(
            src_ref=out[a].at[s], dst_ref=out[a].at[s],
            send_sem=cs.at[a, k, dist - 1, d], recv_sem=cr.at[a, k, dist - 1, d],
            device_id={"mp": x * 2 + 1 - c}, device_id_type=MESH)

    def when(cond, f):
        @pl.when(cond)
        def _():
            f()

    can = {True: z < nz - 1, False: z > 0}

    for a in range(2):
        for right in (True, False):
            when(can[right], lambda a=a, right=right: zsend(a, 0, right).start())
    for a in range(2):
        loads[a].wait()
        st = pltpu.make_async_copy(
            stage.at[a], out[a].at[pl.ds(pl.multiple_of(z * rows, rows), rows)], lsem.at[a])
        st.start()

    def has(dist, right):
        return z - dist >= 0 if right else z + dist <= nz - 1

    def zstep(dist):
        for a in range(2):
            for right in (True, False):
                k = 0 if right else 1

                def got(a=a, right=right, k=k):
                    zrecv(a, dist, right).wait_recv()
                    if dist < nz - 1:
                        when(can[right], lambda: zsend(a, dist, right).start())
                    for d in range(1, nx):
                        xcopy(a, k, dist, d, right, True).start()
                    ccopy(a, k, dist, 0, right, True).start()

                when(has(dist, right), got)

    def xstep(dist):
        for a in range(2):
            for right in (True, False):
                k = 0 if right else 1

                def got(a=a, right=right, k=k):
                    for d in range(1, nx):
                        xcopy(a, k, dist, d, right, False).wait_recv()
                        ccopy(a, k, dist, d, right, True).start()

                when(has(dist, right), got)

    for dist in range(1, nz):
        zstep(dist)
        if dist > 1:
            xstep(dist - 1)
    xstep(nz - 1)

    for a in range(2):
        pltpu.make_async_copy(
            stage.at[a], out[a].at[pl.ds(pl.multiple_of(z * rows, rows), rows)], lsem.at[a]).wait()
    for dist in range(0, nz):
        for a in range(2):
            for right in (True, False):
                k = 0 if right else 1
                if dist < nz - 1:
                    cond = can[right] if dist == 0 else has(dist, right) & can[right]
                    when(cond, lambda a=a, right=right: zsend(a, dist, right).wait_send())
                if dist > 0:
                    def fin(a=a, right=right, k=k):
                        for d in range(1, nx):
                            xcopy(a, k, dist, d, right, True).wait_send()
                        for d in range(nx):
                            ccopy(a, k, dist, d, right, True).wait_send()
                            ccopy(a, k, dist, d, right, False).wait_recv()
                    when(has(dist, right), fin)


def gather_inputs(nuc, loc, nz, nm):
    rows, width = nuc.shape
    nx = nm // 2
    dma = pltpu.SemaphoreType.DMA
    anyspec = pl.BlockSpec(memory_space=pl.ANY)
    shape = jax.ShapeDtypeStruct((nz * rows, width), bf16)
    return pl.pallas_call(
        functools.partial(gather_kernel, nz, nm),
        out_shape=(shape, shape),
        in_specs=[anyspec] * 2,
        out_specs=[anyspec] * 2,
        scratch_shapes=[
            pltpu.VMEM((2, rows, width), bf16),
            dma((2,)),
            dma((2, 2, nz)), dma((2, 2, nz)),
            dma((2, 2, nz - 1, nx)), dma((2, 2, nz - 1, nx)),
            dma((2, 2, nz - 1, nx)), dma((2, 2, nz - 1, nx)),
        ],
        compiler_params=pltpu.CompilerParams(collective_id=0, has_side_effects=True),
        name="gather_inputs",
    )(nuc, loc)


def attend_kernel(nz, heads, qk, vd, sharp, nuc, loc, gain, wqk, wv, out, q_s, k_s, v_s):
    t, j = pl.program_id(0), pl.program_id(1)
    z = lax.axis_index("seq")
    rows = nuc.shape[0]
    b = 128

    def body(flip):
        r_i = lax.broadcasted_iota(jnp.int32, (b, b), 0)
        c_i = lax.broadcasted_iota(jnp.int32, (b, b), 1)
        anti = jnp.where(r_i + c_i == b - 1, 1.0, 0.0).astype(bf16)
        parts = []
        nb = rows // b
        for i in range(nb):
            if flip:
                l = jnp.dot(anti, loc[(nb - 1 - i) * b:(nb - i) * b, :], preferred_element_type=f32)
            else:
                l = loc[i * b:(i + 1) * b, :].astype(f32)
            s = nuc[i * b:(i + 1) * b, :].astype(f32) + l
            parts.append((normalize(s) * gain[...]).astype(bf16))
        normed = jnp.concatenate(parts, axis=0)
        here = pl.ds(pl.multiple_of(j * rows, rows), rows)
        key = jnp.dot(normed, wqk[1], preferred_element_type=f32)
        for h in range(heads):
            k_s[here, h * qk:(h + 1) * qk] = normalize(key[:, h * qk:(h + 1) * qk]).astype(bf16)
        v_s[here, :] = jnp.dot(normed, wv[...], preferred_element_type=f32).astype(bf16)

        @pl.when(j == z)
        def _():
            query = jnp.dot(normed, wqk[0], preferred_element_type=f32)
            for h in range(heads):
                q_s[:, h * qk:(h + 1) * qk] = normalize(query[:, h * qk:(h + 1) * qk]).astype(bf16)

    @pl.when(t == 0)
    def _():
        body(False)

    @pl.when(t == 1)
    def _():
        body(True)

    @pl.when(j == nz - 1)
    def _():
        s_all = k_s.shape[0]
        chunk = 128
        wide = heads * vd
        for i in range(rows // chunk):
            rr = slice(i * chunk, (i + 1) * chunk)
            res = []
            for h in range(heads):
                lo = (h * vd) // 128 * 128
                hi = min(-(-((h + 1) * vd) // 128) * 128, wide)
                num = jnp.zeros((chunk, hi - lo), f32)
                tot = jnp.zeros((chunk, 1), f32)
                step = 1536
                for kk in range(0, s_all, step):
                    sc = lax.dot_general(
                        q_s[rr, h * qk:(h + 1) * qk], k_s[kk:kk + step, h * qk:(h + 1) * qk],
                        (((1,), (1,)), ((), ())), preferred_element_type=f32)
                    w = jnp.exp(sc * (sharp[h] / qk))
                    tot = tot + jnp.sum(w, axis=-1, keepdims=True)
                    num = num + jnp.dot(w.astype(bf16), v_s[kk:kk + step, lo:hi],
                                        preferred_element_type=f32)
                res.append((lo, hi, num / tot))
            if heads == 1:
                out[rr, :] = res[0][2].astype(bf16)
            else:
                for lo in range(0, wide, 128):
                    hi = min(lo + 128, wide)
                    col = lo + lax.broadcasted_iota(jnp.int32, (chunk, hi - lo), 1)
                    val = None
                    for h in range(heads):
                        l0, h0, r = res[h]
                        if h * vd < hi and (h + 1) * vd > lo:
                            v = r[:, lo - l0:hi - l0]
                            val = v if val is None else jnp.where(col < h * vd, val, v)
                    out[rr, lo:hi] = val.astype(bf16)


def attend(nuc_all, loc_all, gain, wqk, wv, sharp, nz, rows):
    heads = sharp.shape[0]
    width = nuc_all.shape[1]
    qk = wqk.shape[2] // heads
    vd = wv.shape[1] // heads
    s_all = nuc_all.shape[0]
    full = lambda a: pl.BlockSpec(a.shape, lambda t, j: (0,) * a.ndim, pipeline_mode=pl.Buffered(1))
    gain = gain.reshape(1, width)
    return pl.pallas_call(
        functools.partial(attend_kernel, nz, heads, qk, vd),
        grid=(2, nz),
        out_shape=jax.ShapeDtypeStruct((2, rows, heads * vd), bf16),
        in_specs=[
            pl.BlockSpec(memory_space=pltpu.SMEM),
            pl.BlockSpec((rows, width), lambda t, j: (j, 0)),
            pl.BlockSpec((rows, width), lambda t, j: (t * (nz - 1 - j) + (1 - t) * j, 0)),
            full(gain), full(wqk), full(wv),
        ],
        out_specs=pl.BlockSpec((pl.Squeezed(), rows, heads * vd), lambda t, j: (t, 0, 0)),
        scratch_shapes=[
            pltpu.VMEM((rows, heads * qk), bf16),
            pltpu.VMEM((s_all, heads * qk), bf16),
            pltpu.VMEM((s_all, heads * vd), bf16),
        ],
        compiler_params=pltpu.CompilerParams(vmem_limit_bytes=56 << 20),
        name="attend",
    )(sharp, nuc_all, loc_all, gain, wqk, wv)


def spread_kernel(nm, parts, src, out, lsem, xs, xr, cs, cr):
    nx = nm // 2
    m = lax.axis_index("mp")
    x, c = m // 2, m % 2
    n = src.shape[0] // parts
    barrier = pltpu.get_barrier_semaphore()
    for d in range(1, nx):
        pl.semaphore_signal(barrier, inc=1, device_id={"mp": lax.rem(x + d, nx) * 2 + c}, device_id_type=MESH)
    pl.semaphore_signal(barrier, inc=1, device_id={"mp": x * 2 + 1 - c}, device_id_type=MESH)
    local = pltpu.make_async_copy(src, out.at[m], lsem)
    local.start()
    pl.semaphore_wait(barrier, nx)

    def xcopy(i, d, mine):
        o = lax.rem(x + d, nx) if mine else lax.rem(x - d + nx, nx)
        k = m if mine else o * 2 + c
        r = pl.ds(i * n, n)
        return pltpu.make_async_remote_copy(
            src_ref=src.at[r], dst_ref=out.at[k, r], send_sem=xs.at[i, d - 1],
            recv_sem=xr.at[i, d - 1], device_id={"mp": o * 2 + c}, device_id_type=MESH)

    def ccopy(i, d, mine):
        o = lax.rem(x - d + nx, nx)
        k = o * 2 + (c if mine else 1 - c)
        r = pl.ds(i * n, n)
        ref = src.at[r] if d == 0 else out.at[k, r]
        return pltpu.make_async_remote_copy(
            src_ref=ref, dst_ref=out.at[k, r], send_sem=cs.at[i, d], recv_sem=cr.at[i, d],
            device_id={"mp": x * 2 + 1 - c}, device_id_type=MESH)

    for i in range(parts):
        for d in range(1, nx):
            xcopy(i, d, True).start()
    for i in range(parts):
        ccopy(i, 0, True).start()
    for i in range(parts):
        for d in range(1, nx):
            xcopy(i, d, False).wait_recv()
            ccopy(i, d, True).start()
    local.wait()
    for i in range(parts):
        for d in range(1, nx):
            xcopy(i, d, True).wait_send()
        for d in range(nx):
            ccopy(i, d, True).wait_send()
            ccopy(i, d, False).wait_recv()


def spread(a, nm, parts=4):
    nx = nm // 2
    dma = pltpu.SemaphoreType.DMA
    vm = pl.BlockSpec(memory_space=pltpu.VMEM)
    return pl.pallas_call(
        functools.partial(spread_kernel, nm, parts),
        out_shape=jax.ShapeDtypeStruct((nm,) + a.shape, a.dtype),
        in_specs=[vm],
        out_specs=vm,
        scratch_shapes=[dma, dma((parts, nx)), dma((parts, nx)), dma((parts, nx)), dma((parts, nx))],
        compiler_params=pltpu.CompilerParams(
            collective_id=1, has_side_effects=True, vmem_limit_bytes=40 << 20),
        name="spread",
    )(a)


def shards(nuc, loc, premix, wqk, wv, sharp, mixing, premlp, widen, narrow):
    rows, width = nuc.shape
    nz, nm = lax.axis_size("seq"), lax.axis_size("mp")
    z = lax.axis_index("seq")
    nuc_all, loc_all = gather_inputs(nuc, loc, nz, nm)
    mixing, nuc_all, loc_all = lax.optimization_barrier((mixing, nuc_all, loc_all))
    mix_all = lax.all_gather(mixing, "mp", axis=0, tiled=False)
    att = attend(nuc_all, loc_all, premix, wqk, wv, sharp, nz, rows)
    att_all = spread(att.reshape(2 * rows, -1), nm)
    loc_m = lax.dynamic_slice_in_dim(loc_all, (nz - 1 - z) * rows, rows, 0)
    i = lax.broadcasted_iota(jnp.int32, (rows, rows), 0)
    k = lax.broadcasted_iota(jnp.int32, (rows, rows), 1)
    anti = (i + k == rows - 1).astype(bf16)
    loc_rev = jnp.dot(anti, loc_m, preferred_element_type=f32)
    nf = nuc.astype(f32)
    stream = jnp.concatenate([nf + loc.astype(f32), nf + loc_rev], axis=0)
    proj = jnp.einsum("mrc,mcd->rd", att_all, mix_all, preferred_element_type=f32)
    middle = stream + proj
    normed_mid = (normalize(middle) * premlp).astype(bf16)
    up = jnp.dot(normed_mid, widen, preferred_element_type=f32)
    g = jax.nn.gelu(up, approximate=True)
    both = (g[:rows] + g[rows:]).astype(bf16)
    down = jnp.dot(both, narrow, preferred_element_type=f32)
    red = lax.psum_scatter(down.astype(bf16), "mp", scatter_dimension=1, tiled=True).astype(f32)
    share = width // nm
    mid = lax.dynamic_slice_in_dim(middle[:rows] + middle[rows:], lax.axis_index("mp") * share, share, 1)
    return 0.5 * (mid + red)


def solution(mesh):
    return jax.shard_map(
        shards,
        mesh=mesh,
        in_specs=(
            P(("groups", "seq"), None),
            P("seq", None),
            P(),
            P(None, None, "mp"),
            P(None, "mp"),
            P("mp"),
            P("mp", None),
            P(),
            P(None, "mp"),
            P("mp", None),
        ),
        out_specs=P(("groups", "seq"), "mp"),
        check_vma=False,
    )
```

```python
import functools

import jax
import jax.numpy as jnp
from jax import lax
from jax.experimental import pallas as pl
from jax.experimental.pallas import tpu as pltpu
from jax.sharding import PartitionSpec as P

epsilon = 1e-06
MESH = pl.DeviceIdType.MESH
f32 = jnp.float32
bf16 = jnp.bfloat16


def normalize(v):
    return v * lax.rsqrt(jnp.mean(v * v, axis=-1, keepdims=True) + epsilon)


def gather_kernel(nz, nm, *refs):
    src = refs[0:2]
    out = refs[2:4]
    stage, lsem, zs, zr, xs, xr, cs, cr = refs[4:]
    nx = nm // 2
    z = lax.axis_index("seq")
    m = lax.axis_index("mp")
    x, c = m // 2, m % 2
    rows = src[0].shape[0]
    piece = rows // nm

    def at(zsrc, mm):
        return pl.ds(pl.multiple_of(zsrc * rows + mm * piece, piece), piece)

    others = [lax.rem(x + d, nx) for d in range(1, nx)]
    barrier = pltpu.get_barrier_semaphore()

    @pl.when(z > 0)
    def _():
        pl.semaphore_signal(barrier, inc=1, device_id={"seq": z - 1}, device_id_type=MESH)

    @pl.when(z < nz - 1)
    def _():
        pl.semaphore_signal(barrier, inc=1, device_id={"seq": z + 1}, device_id_type=MESH)

    for o in others:
        pl.semaphore_signal(barrier, inc=1, device_id={"mp": o * 2 + c}, device_id_type=MESH)
    pl.semaphore_signal(barrier, inc=1, device_id={"mp": x * 2 + 1 - c}, device_id_type=MESH)

    loads = [pltpu.make_async_copy(src[a], stage.at[a], lsem.at[a]) for a in range(2)]
    for cp in loads:
        cp.start()

    pl.semaphore_wait(barrier, nx + jnp.where(z > 0, 1, 0) + jnp.where(z < nz - 1, 1, 0))

    def zsend(a, dist, right):
        zsrc = z - dist if right else z + dist
        s = at(zsrc, m)
        if dist == 0:
            ref = src[a].at[pl.ds(pl.multiple_of(m * piece, piece), piece)]
        else:
            ref = out[a].at[s]
        k = 0 if right else 1
        return pltpu.make_async_remote_copy(
            src_ref=ref, dst_ref=out[a].at[s],
            send_sem=zs.at[a, k, dist], recv_sem=zr.at[a, k, dist],
            device_id={"seq": z + 1 if right else z - 1}, device_id_type=MESH)

    def zrecv(a, dist, right):
        zsrc = z - dist if right else z + dist
        s = at(zsrc, m)
        k = 0 if right else 1
        return pltpu.make_async_remote_copy(
            src_ref=out[a].at[s], dst_ref=out[a].at[s],
            send_sem=zs.at[a, k, dist - 1], recv_sem=zr.at[a, k, dist - 1],
            device_id={"seq": z + 1 if right else z - 1}, device_id_type=MESH)

    def xcopy(a, k, dist, d, right, mine):
        zsrc = z - dist if right else z + dist
        o = lax.rem(x + d, nx) if mine else lax.rem(x - d + nx, nx)
        s = at(zsrc, m if mine else o * 2 + c)
        return pltpu.make_async_remote_copy(
            src_ref=out[a].at[s], dst_ref=out[a].at[s],
            send_sem=xs.at[a, k, dist - 1, d - 1], recv_sem=xr.at[a, k, dist - 1, d - 1],
            device_id={"mp": o * 2 + c}, device_id_type=MESH)

    def ccopy(a, k, dist, d, right, mine):
        zsrc = z - dist if right else z + dist
        o = lax.rem(x - d + nx, nx)
        s = at(zsrc, o * 2 + (c if mine else 1 - c))
        return pltpu.make_async_remote_copy(
            src_ref=out[a].at[s], dst_ref=out[a].at[s],
            send_sem=cs.at[a, k, dist - 1, d], recv_sem=cr.at[a, k, dist - 1, d],
            device_id={"mp": x * 2 + 1 - c}, device_id_type=MESH)

    def when(cond, f):
        @pl.when(cond)
        def _():
            f()

    can = {True: z < nz - 1, False: z > 0}

    for a in range(2):
        for right in (True, False):
            when(can[right], lambda a=a, right=right: zsend(a, 0, right).start())
    for a in range(2):
        loads[a].wait()
        st = pltpu.make_async_copy(
            stage.at[a], out[a].at[pl.ds(pl.multiple_of(z * rows, rows), rows)], lsem.at[a])
        st.start()

    def has(dist, right):
        return z - dist >= 0 if right else z + dist <= nz - 1

    def zstep(dist):
        for a in range(2):
            for right in (True, False):
                k = 0 if right else 1

                def got(a=a, right=right, k=k):
                    zrecv(a, dist, right).wait_recv()
                    if dist < nz - 1:
                        when(can[right], lambda: zsend(a, dist, right).start())
                    for d in range(1, nx):
                        xcopy(a, k, dist, d, right, True).start()
                    ccopy(a, k, dist, 0, right, True).start()

                when(has(dist, right), got)

    def xstep(dist):
        for a in range(2):
            for right in (True, False):
                k = 0 if right else 1

                def got(a=a, right=right, k=k):
                    for d in range(1, nx):
                        xcopy(a, k, dist, d, right, False).wait_recv()
                        ccopy(a, k, dist, d, right, True).start()

                when(has(dist, right), got)

    for dist in range(1, nz):
        zstep(dist)
        if dist > 1:
            xstep(dist - 1)
    xstep(nz - 1)

    for a in range(2):
        pltpu.make_async_copy(
            stage.at[a], out[a].at[pl.ds(pl.multiple_of(z * rows, rows), rows)], lsem.at[a]).wait()
    for dist in range(0, nz):
        for a in range(2):
            for right in (True, False):
                k = 0 if right else 1
                if dist < nz - 1:
                    cond = can[right] if dist == 0 else has(dist, right) & can[right]
                    when(cond, lambda a=a, right=right: zsend(a, dist, right).wait_send())
                if dist > 0:
                    def fin(a=a, right=right, k=k):
                        for d in range(1, nx):
                            xcopy(a, k, dist, d, right, True).wait_send()
                        for d in range(nx):
                            ccopy(a, k, dist, d, right, True).wait_send()
                            ccopy(a, k, dist, d, right, False).wait_recv()
                    when(has(dist, right), fin)


def gather_inputs(nuc, loc, nz, nm):
    rows, width = nuc.shape
    nx = nm // 2
    dma = pltpu.SemaphoreType.DMA
    anyspec = pl.BlockSpec(memory_space=pl.ANY)
    shape = jax.ShapeDtypeStruct((nz * rows, width), bf16)
    return pl.pallas_call(
        functools.partial(gather_kernel, nz, nm),
        out_shape=(shape, shape),
        in_specs=[anyspec] * 2,
        out_specs=[anyspec] * 2,
        scratch_shapes=[
            pltpu.VMEM((2, rows, width), bf16),
            dma((2,)),
            dma((2, 2, nz)), dma((2, 2, nz)),
            dma((2, 2, nz - 1, nx)), dma((2, 2, nz - 1, nx)),
            dma((2, 2, nz - 1, nx)), dma((2, 2, nz - 1, nx)),
        ],
        compiler_params=pltpu.CompilerParams(collective_id=0, has_side_effects=True),
        name="gather_inputs",
    )(nuc, loc)


def attend_kernel(nz, nm, heads, qk, vd, sharp, nuc, loc, gain, wqk, wv, mix, out, mix_all,
                  q_s, k_s, v_s, xs, xr, ys, yr, cs, cr, os, orr):
    share_mix(nz, nm, mix, mix_all, xs, xr, ys, yr, cs, cr, os, orr, 0)
    t, j = pl.program_id(0), pl.program_id(1)
    z = lax.axis_index("seq")
    rows = nuc.shape[0]
    b = 128

    def body(flip):
        r_i = lax.broadcasted_iota(jnp.int32, (b, b), 0)
        c_i = lax.broadcasted_iota(jnp.int32, (b, b), 1)
        anti = jnp.where(r_i + c_i == b - 1, 1.0, 0.0).astype(bf16)
        parts = []
        nb = rows // b
        for i in range(nb):
            if flip:
                l = jnp.dot(anti, loc[(nb - 1 - i) * b:(nb - i) * b, :], preferred_element_type=f32)
            else:
                l = loc[i * b:(i + 1) * b, :].astype(f32)
            s = nuc[i * b:(i + 1) * b, :].astype(f32) + l
            parts.append((normalize(s) * gain[...]).astype(bf16))
        normed = jnp.concatenate(parts, axis=0)
        here = pl.ds(pl.multiple_of(j * rows, rows), rows)
        key = jnp.dot(normed, wqk[1], preferred_element_type=f32)
        for h in range(heads):
            k_s[here, h * qk:(h + 1) * qk] = normalize(key[:, h * qk:(h + 1) * qk]).astype(bf16)
        v_s[here, :] = jnp.dot(normed, wv[...], preferred_element_type=f32).astype(bf16)

        @pl.when(j == z)
        def _():
            query = jnp.dot(normed, wqk[0], preferred_element_type=f32)
            for h in range(heads):
                q_s[:, h * qk:(h + 1) * qk] = normalize(query[:, h * qk:(h + 1) * qk]).astype(bf16)

    @pl.when(t == 0)
    def _():
        body(False)

    @pl.when(t == 1)
    def _():
        body(True)

    @pl.when(j == nz - 1)
    def _():
        s_all = k_s.shape[0]
        chunk = 128
        wide = heads * vd
        for i in range(rows // chunk):
            rr = slice(i * chunk, (i + 1) * chunk)
            res = []
            for h in range(heads):
                lo = (h * vd) // 128 * 128
                hi = min(-(-((h + 1) * vd) // 128) * 128, wide)
                num = jnp.zeros((chunk, hi - lo), f32)
                tot = jnp.zeros((chunk, 1), f32)
                step = 1536
                for kk in range(0, s_all, step):
                    sc = lax.dot_general(
                        q_s[rr, h * qk:(h + 1) * qk], k_s[kk:kk + step, h * qk:(h + 1) * qk],
                        (((1,), (1,)), ((), ())), preferred_element_type=f32)
                    w = jnp.exp(sc * (sharp[h] / qk))
                    tot = tot + jnp.sum(w, axis=-1, keepdims=True)
                    num = num + jnp.dot(w.astype(bf16), v_s[kk:kk + step, lo:hi],
                                        preferred_element_type=f32)
                res.append((lo, hi, num / tot))
            if heads == 1:
                out[rr, :] = res[0][2].astype(bf16)
            else:
                for lo in range(0, wide, 128):
                    hi = min(lo + 128, wide)
                    col = lo + lax.broadcasted_iota(jnp.int32, (chunk, hi - lo), 1)
                    val = None
                    for h in range(heads):
                        l0, h0, r = res[h]
                        if h * vd < hi and (h + 1) * vd > lo:
                            v = r[:, lo - l0:hi - l0]
                            val = v if val is None else jnp.where(col < h * vd, val, v)
                    out[rr, lo:hi] = val.astype(bf16)

    share_mix(nz, nm, mix, mix_all, xs, xr, ys, yr, cs, cr, os, orr, 1)


def share_mix(nz, nm, mix, mix_all, xs, xr, ys, yr, cs, cr, os, orr, phase):
    nx = nm // 2
    step = pl.program_id(0) * nz + pl.program_id(1)
    m = lax.axis_index("mp")
    g = lax.axis_index("groups")
    x, c = m // 2, m % 2
    size = mix.shape[0] // 4

    def rows(gg, p):
        return pl.ds(pl.multiple_of((gg * 2 + p) * size, size), size)

    def xcopy(p, d, mine):
        o = lax.rem(x + d, nx) if mine else lax.rem(x - d + nx, nx)
        k = m if mine else o * 2 + c
        return pltpu.make_async_remote_copy(
            src_ref=mix.at[rows(g, p)], dst_ref=mix_all.at[k, rows(g, p)],
            send_sem=xs.at[p, d - 1], recv_sem=xr.at[p, d - 1],
            device_id={"mp": o * 2 + c}, device_id_type=MESH)

    def ycopy(p, d, mine):
        k = lax.rem(x - d + nx, nx) * 2 + c
        r = rows(g if mine else 1 - g, p)
        return pltpu.make_async_remote_copy(
            src_ref=mix_all.at[k, r], dst_ref=mix_all.at[k, r],
            send_sem=ys.at[p, d - 1], recv_sem=yr.at[p, d - 1],
            device_id={"groups": 1 - g}, device_id_type=MESH)

    def ccopy(p, d, far, mine):
        k = lax.rem(x - d + nx, nx) * 2 + (c if mine else 1 - c)
        r = rows(1 - g if far else g, p)
        f = 1 if far else 0
        return pltpu.make_async_remote_copy(
            src_ref=mix_all.at[k, r], dst_ref=mix_all.at[k, r],
            send_sem=cs.at[p, d - 1, f], recv_sem=cr.at[p, d - 1, f],
            device_id={"mp": x * 2 + 1 - c}, device_id_type=MESH)

    def own(mine):
        return pltpu.make_async_remote_copy(
            src_ref=mix, dst_ref=mix_all.at[m if mine else x * 2 + 1 - c],
            send_sem=os, recv_sem=orr,
            device_id={"mp": x * 2 + 1 - c}, device_id_type=MESH)

    if phase == 0:
        @pl.when(step == 0)
        def _():
            barrier = pltpu.get_barrier_semaphore()
            for d in range(1, nx):
                pl.semaphore_signal(barrier, inc=1, device_id={"mp": lax.rem(x + d, nx) * 2 + c}, device_id_type=MESH)
            pl.semaphore_signal(barrier, inc=1, device_id={"mp": x * 2 + 1 - c}, device_id_type=MESH)
            pl.semaphore_signal(barrier, inc=1, device_id={"groups": 1 - g}, device_id_type=MESH)
            pl.semaphore_wait(barrier, nx + 1)
            for p in range(2):
                for d in range(1, nx):
                    xcopy(p, d, True).start()
            own(True).start()

        for p in range(2):
            @pl.when(step == nz + 2 * p)
            def _(p=p):
                for d in range(1, nx):
                    xcopy(p, d, False).wait_recv()
                    ycopy(p, d, True).start()
                    ccopy(p, d, False, True).start()
    else:
        @pl.when(step == 2 * nz - 1)
        def _():
            for p in range(2):
                for d in range(1, nx):
                    ycopy(p, d, False).wait_recv()
                    ccopy(p, d, True, True).start()
            own(True).wait_send()
            own(False).wait_recv()
            for p in range(2):
                for d in range(1, nx):
                    xcopy(p, d, True).wait_send()
                    ycopy(p, d, True).wait_send()
                    for far in (False, True):
                        ccopy(p, d, far, True).wait_send()
                        ccopy(p, d, far, False).wait_recv()


def attend(nuc_all, loc_all, gain, wqk, wv, sharp, mix, nz, nm, rows):
    heads = sharp.shape[0]
    width = nuc_all.shape[1]
    qk = wqk.shape[2] // heads
    vd = wv.shape[1] // heads
    s_all = nuc_all.shape[0]
    nx = nm // 2
    dma = pltpu.SemaphoreType.DMA
    full = lambda a: pl.BlockSpec(a.shape, lambda t, j: (0,) * a.ndim, pipeline_mode=pl.Buffered(1))
    anyspec = pl.BlockSpec(memory_space=pl.ANY)
    gain = gain.reshape(1, width)
    return pl.pallas_call(
        functools.partial(attend_kernel, nz, nm, heads, qk, vd),
        grid=(2, nz),
        out_shape=(jax.ShapeDtypeStruct((2, rows, heads * vd), bf16),
                   jax.ShapeDtypeStruct((nm,) + mix.shape, bf16)),
        in_specs=[
            pl.BlockSpec(memory_space=pltpu.SMEM),
            pl.BlockSpec((rows, width), lambda t, j: (j, 0)),
            pl.BlockSpec((rows, width), lambda t, j: (t * (nz - 1 - j) + (1 - t) * j, 0)),
            full(gain), full(wqk), full(wv), anyspec,
        ],
        out_specs=(pl.BlockSpec((pl.Squeezed(), rows, heads * vd), lambda t, j: (t, 0, 0)), anyspec),
        scratch_shapes=[
            pltpu.VMEM((rows, heads * qk), bf16),
            pltpu.VMEM((s_all, heads * qk), bf16),
            pltpu.VMEM((s_all, heads * vd), bf16),
            dma((2, nx)), dma((2, nx)), dma((2, nx)), dma((2, nx)),
            dma((2, nx, 2)), dma((2, nx, 2)), dma, dma,
        ],
        compiler_params=pltpu.CompilerParams(
            collective_id=2, has_side_effects=True, vmem_limit_bytes=56 << 20),
        name="attend",
    )(sharp, nuc_all, loc_all, gain, wqk, wv, mix)


def tail_kernel(nz, nm, att, nuc_h, loc_h, loc_all, gain, mix, mix_all, widen_h, narrow_h, out,
                att_all, nuc, loc, locm, mixv, widen, narrow, sbuf, rbuf, mid,
                lsem, msem, xs, xr, cs, cr, ss, sr):
    nx = nm // 2
    rows, width = nuc.shape
    share = width // nm
    b = 128
    parts = rows // b
    z = lax.axis_index("seq")
    m = lax.axis_index("mp")
    x, c = m // 2, m % 2
    barrier = pltpu.get_barrier_semaphore()
    for d in range(1, nm):
        pl.semaphore_signal(barrier, inc=1, device_id={"mp": lax.rem(m + d, nm)}, device_id_type=MESH)
    loads = [
        pltpu.make_async_copy(att, att_all.at[m], lsem.at[0]),
        pltpu.make_async_copy(nuc_h, nuc, lsem.at[1]),
        pltpu.make_async_copy(loc_h, loc, lsem.at[2]),
        pltpu.make_async_copy(loc_all.at[pl.ds(pl.multiple_of((nz - 1 - z) * rows, rows), rows)], locm, lsem.at[3]),
        pltpu.make_async_copy(widen_h, widen, lsem.at[4]),
        pltpu.make_async_copy(narrow_h, narrow, lsem.at[5]),
    ]
    mloads = [pltpu.make_async_copy(mix, mixv.at[m], msem.at[0])]
    for d in range(1, nm):
        k = lax.rem(m + d, nm)
        mloads.append(pltpu.make_async_copy(mix_all.at[k], mixv.at[k], msem.at[d]))
    for cp in loads[:4] + mloads + loads[4:]:
        cp.start()
    pl.semaphore_wait(barrier, nm - 1)

    def xcopy(i, d, mine):
        o = lax.rem(x + d, nx) if mine else lax.rem(x - d + nx, nx)
        k = m if mine else o * 2 + c
        r = pl.ds(i * b, b)
        return pltpu.make_async_remote_copy(
            src_ref=att.at[:, r], dst_ref=att_all.at[k, :, r], send_sem=xs.at[i, d - 1],
            recv_sem=xr.at[i, d - 1], device_id={"mp": o * 2 + c}, device_id_type=MESH)

    def ccopy(i, d, mine):
        o = lax.rem(x - d + nx, nx)
        k = o * 2 + (c if mine else 1 - c)
        r = pl.ds(i * b, b)
        ref = att.at[:, r] if d == 0 else att_all.at[k, :, r]
        return pltpu.make_async_remote_copy(
            src_ref=ref, dst_ref=att_all.at[k, :, r], send_sem=cs.at[i, d], recv_sem=cr.at[i, d],
            device_id={"mp": x * 2 + 1 - c}, device_id_type=MESH)

    def scopy(i, d):
        k = lax.rem(m + d, nm)
        return pltpu.make_async_remote_copy(
            src_ref=sbuf.at[i, k], dst_ref=rbuf.at[i, d - 1], send_sem=ss.at[i, d - 1],
            recv_sem=sr.at[i, d - 1], device_id={"mp": k}, device_id_type=MESH)

    for i in range(parts):
        for d in range(1, nx):
            xcopy(i, d, True).start()
        ccopy(i, 0, True).start()

    def pass_on(i):
        for d in range(1, nx):
            xcopy(i, d, False).wait_recv()
            ccopy(i, d, True).start()

    r_i = lax.broadcasted_iota(jnp.int32, (b, b), 0)
    c_i = lax.broadcasted_iota(jnp.int32, (b, b), 1)
    anti = jnp.where(r_i + c_i == b - 1, 1.0, 0.0).astype(bf16)
    for cp in loads[:4]:
        cp.wait()
    pass_on(0)
    for cp in mloads:
        cp.wait()
    for i in range(parts):
        r = slice(i * b, (i + 1) * b)
        n = nuc[r, :].astype(f32)
        s0 = n + loc[r, :].astype(f32)
        s1 = n + jnp.dot(anti, locm[(parts - 1 - i) * b:(parts - i) * b, :], preferred_element_type=f32)
        middle = jnp.concatenate([s0, s1], axis=0)
        for d in range(nx):
            ccopy(i, d, False).wait_recv()
        for k in range(nm):
            a = jnp.concatenate([att_all[k, 0, r, :], att_all[k, 1, r, :]], axis=0)
            middle = middle + jnp.dot(a, mixv[k], preferred_element_type=f32)
        if i + 1 < parts:
            pass_on(i + 1)
        normed = (normalize(middle) * gain[...]).astype(bf16)
        if i == 0:
            for cp in loads[4:]:
                cp.wait()
        up = jax.nn.gelu(jnp.dot(normed, widen[...], preferred_element_type=f32), approximate=True)
        both = (up[:b] + up[b:]).astype(bf16)
        down = jnp.dot(both, narrow[...], preferred_element_type=f32)
        total = middle[:b] + middle[b:] + down
        down = down.astype(bf16)
        for k in range(nm):
            sbuf[i, k] = down[:, k * share:(k + 1) * share]
            mid[i, k] = total[:, k * share:(k + 1) * share]
        for d in range(1, nm):
            scopy(i, d).start()
    for i in range(parts):
        acc = mid[i, m]
        for d in range(1, nm):
            scopy(i, d).wait_recv()
            acc = acc + rbuf[i, d - 1].astype(f32)
        out[i * b:(i + 1) * b, :] = 0.5 * acc
    for i in range(parts):
        for d in range(1, nx):
            xcopy(i, d, True).wait_send()
        for d in range(nx):
            ccopy(i, d, True).wait_send()
        for d in range(1, nm):
            scopy(i, d).wait_send()


def tail(att, nuc, loc, loc_all, gain, mix, mix_all, widen, narrow, nz, nm):
    rows, width = nuc.shape
    share = width // nm
    nx = nm // 2
    parts = rows // 128
    dma = pltpu.SemaphoreType.DMA
    anyspec = pl.BlockSpec(memory_space=pl.ANY)
    vm = pl.BlockSpec(memory_space=pltpu.VMEM)
    v = pltpu.VMEM
    return pl.pallas_call(
        functools.partial(tail_kernel, nz, nm),
        out_shape=jax.ShapeDtypeStruct((rows, share), f32),
        in_specs=[vm, anyspec, anyspec, anyspec, vm, anyspec, anyspec, anyspec, anyspec],
        out_specs=vm,
        scratch_shapes=[
            v((nm,) + att.shape, bf16), v(nuc.shape, bf16), v(nuc.shape, bf16), v(nuc.shape, bf16),
            v((nm,) + mix.shape, bf16), v(widen.shape, bf16), v(narrow.shape, bf16),
            v((parts, nm, 128, share), bf16), v((parts, nm - 1, 128, share), bf16),
            v((parts, nm, 128, share), f32),
            dma((6,)), dma((nm,)),
            dma((parts, nx)), dma((parts, nx)), dma((parts, nx)), dma((parts, nx)),
            dma((parts, nm)), dma((parts, nm)),
        ],
        compiler_params=pltpu.CompilerParams(
            collective_id=3, has_side_effects=True, vmem_limit_bytes=56 << 20),
        name="tail",
    )(att, nuc, loc, loc_all, gain.reshape(1, width), mix, mix_all, widen, narrow)


def shards(nuc, loc, premix, wqk, wv, sharp, mixing, premlp, widen, narrow):
    rows = nuc.shape[0]
    nz, nm = lax.axis_size("seq"), lax.axis_size("mp")
    nuc_all, loc_all = gather_inputs(nuc, loc, nz, nm)
    att, mix_all = attend(nuc_all, loc_all, premix, wqk, wv, sharp, mixing, nz, nm, rows)
    return tail(att, nuc, loc, loc_all, premlp, mixing, mix_all, widen, narrow, nz, nm)


def solution(mesh):
    return jax.shard_map(
        shards,
        mesh=mesh,
        in_specs=(
            P(("groups", "seq"), None),
            P("seq", None),
            P(),
            P(None, None, "mp"),
            P(None, "mp"),
            P("mp"),
            P("mp", None),
            P(),
            P(None, "mp"),
            P("mp", None),
        ),
        out_specs=P(("groups", "seq"), "mp"),
        check_vma=False,
    )
```

```python
import functools

import jax
import jax.numpy as jnp
from jax import lax
from jax.experimental import pallas as pl
from jax.experimental.pallas import tpu as pltpu
from jax.sharding import PartitionSpec as P

epsilon = 1e-06
MESH = pl.DeviceIdType.MESH
f32 = jnp.float32
bf16 = jnp.bfloat16


def normalize(v):
    return v * lax.rsqrt(jnp.mean(v * v, axis=-1, keepdims=True) + epsilon)


def halves(rows, nm):
    return rows // nm % 32 == 0


def gather_kernel(nz, nm, *refs):
    src = refs[0:2]
    out = refs[2:4]
    stage, lsem, zs, zr, xs, xr, cs, cr, ys, yr, fs, fr = refs[4:]
    g = lax.axis_index("groups")
    nx = nm // 2
    z = lax.axis_index("seq")
    m = lax.axis_index("mp")
    x, c = m // 2, m % 2
    rows = src[0].shape[0]
    piece = rows // nm

    split = halves(rows, nm)
    half = piece // 2

    def at(a, zsrc, mm, peer=False):
        if a == 1 and split:
            gg = 1 - g if peer else g
            return pl.ds(pl.multiple_of(zsrc * rows + mm * piece + gg * half, half), half)
        return pl.ds(pl.multiple_of(zsrc * rows + mm * piece, piece), piece)

    others = [lax.rem(x + d, nx) for d in range(1, nx)]
    barrier = pltpu.get_barrier_semaphore()

    @pl.when(z > 0)
    def _():
        pl.semaphore_signal(barrier, inc=1, device_id={"seq": z - 1}, device_id_type=MESH)

    @pl.when(z < nz - 1)
    def _():
        pl.semaphore_signal(barrier, inc=1, device_id={"seq": z + 1}, device_id_type=MESH)

    for o in others:
        pl.semaphore_signal(barrier, inc=1, device_id={"mp": o * 2 + c}, device_id_type=MESH)
    pl.semaphore_signal(barrier, inc=1, device_id={"mp": x * 2 + 1 - c}, device_id_type=MESH)
    if split:
        pl.semaphore_signal(barrier, inc=1, device_id={"groups": 1 - g}, device_id_type=MESH)

    loads = [pltpu.make_async_copy(src[a], stage.at[a], lsem.at[a]) for a in range(2)]
    for cp in loads:
        cp.start()

    pl.semaphore_wait(barrier, nx + int(split) + jnp.where(z > 0, 1, 0) + jnp.where(z < nz - 1, 1, 0))

    def zsend(a, dist, right):
        zsrc = z - dist if right else z + dist
        s = at(a, zsrc, m)
        if dist == 0:
            ref = src[a].at[at(a, 0, m)]
        else:
            ref = out[a].at[s]
        k = 0 if right else 1
        return pltpu.make_async_remote_copy(
            src_ref=ref, dst_ref=out[a].at[s],
            send_sem=zs.at[a, k, dist], recv_sem=zr.at[a, k, dist],
            device_id={"seq": z + 1 if right else z - 1}, device_id_type=MESH)

    def zrecv(a, dist, right):
        zsrc = z - dist if right else z + dist
        s = at(a, zsrc, m)
        k = 0 if right else 1
        return pltpu.make_async_remote_copy(
            src_ref=out[a].at[s], dst_ref=out[a].at[s],
            send_sem=zs.at[a, k, dist - 1], recv_sem=zr.at[a, k, dist - 1],
            device_id={"seq": z + 1 if right else z - 1}, device_id_type=MESH)

    def xcopy(a, k, dist, d, right, mine):
        zsrc = z - dist if right else z + dist
        o = lax.rem(x + d, nx) if mine else lax.rem(x - d + nx, nx)
        s = at(a, zsrc, m if mine else o * 2 + c)
        return pltpu.make_async_remote_copy(
            src_ref=out[a].at[s], dst_ref=out[a].at[s],
            send_sem=xs.at[a, k, dist - 1, d - 1], recv_sem=xr.at[a, k, dist - 1, d - 1],
            device_id={"mp": o * 2 + c}, device_id_type=MESH)

    def ccopy(a, k, dist, d, right, mine):
        zsrc = z - dist if right else z + dist
        o = lax.rem(x - d + nx, nx)
        s = at(a, zsrc, o * 2 + (c if mine else 1 - c))
        return pltpu.make_async_remote_copy(
            src_ref=out[a].at[s], dst_ref=out[a].at[s],
            send_sem=cs.at[a, k, dist - 1, d], recv_sem=cr.at[a, k, dist - 1, d],
            device_id={"mp": x * 2 + 1 - c}, device_id_type=MESH)

    def ycopy(k, dist, d, right, mine):
        zsrc = z - dist if right else z + dist
        s = at(1, zsrc, lax.rem(x - d + nx, nx) * 2 + c, not mine)
        return pltpu.make_async_remote_copy(
            src_ref=out[1].at[s], dst_ref=out[1].at[s],
            send_sem=ys.at[k, dist - 1, d], recv_sem=yr.at[k, dist - 1, d],
            device_id={"groups": 1 - g}, device_id_type=MESH)

    def fcopy(k, dist, d, right, mine):
        zsrc = z - dist if right else z + dist
        s = at(1, zsrc, lax.rem(x - d + nx, nx) * 2 + (c if mine else 1 - c), True)
        return pltpu.make_async_remote_copy(
            src_ref=out[1].at[s], dst_ref=out[1].at[s],
            send_sem=fs.at[k, dist - 1, d], recv_sem=fr.at[k, dist - 1, d],
            device_id={"mp": x * 2 + 1 - c}, device_id_type=MESH)

    def when(cond, f):
        @pl.when(cond)
        def _():
            f()

    can = {True: z < nz - 1, False: z > 0}

    for a in (1, 0):
        for right in (True, False):
            when(can[right], lambda a=a, right=right: zsend(a, 0, right).start())
    for a in range(2):
        loads[a].wait()
        st = pltpu.make_async_copy(
            stage.at[a], out[a].at[pl.ds(pl.multiple_of(z * rows, rows), rows)], lsem.at[a])
        st.start()

    def has(dist, right):
        return z - dist >= 0 if right else z + dist <= nz - 1

    def zstep(dist):
        for a in (1, 0):
            for right in (True, False):
                k = 0 if right else 1

                def got(a=a, right=right, k=k):
                    zrecv(a, dist, right).wait_recv()
                    if dist < nz - 1:
                        when(can[right], lambda: zsend(a, dist, right).start())
                    for d in range(1, nx):
                        xcopy(a, k, dist, d, right, True).start()
                    if a == 1 and split:
                        ycopy(k, dist, 0, right, True).start()
                    ccopy(a, k, dist, 0, right, True).start()

                when(has(dist, right), got)

    def xstep(dist):
        for a in (1, 0):
            for right in (True, False):
                k = 0 if right else 1

                def got(a=a, right=right, k=k):
                    for d in range(1, nx):
                        xcopy(a, k, dist, d, right, False).wait_recv()
                        if a == 1 and split:
                            ycopy(k, dist, d, right, True).start()
                        ccopy(a, k, dist, d, right, True).start()

                when(has(dist, right), got)

    def ystep(dist, ds):
        if not split or dist < 1:
            return
        for right in (True, False):
            k = 0 if right else 1

            def got(right=right, k=k):
                for d in ds:
                    ycopy(k, dist, d, right, False).wait_recv()
                    fcopy(k, dist, d, right, True).start()

            when(has(dist, right), got)

    far = tuple(range(1, nx))
    for dist in range(1, nz):
        zstep(dist)
        if dist > 1:
            xstep(dist - 1)
        ystep(dist - 1, (0,))
        ystep(dist - 2, far)
    ystep(nz - 2, far)
    ystep(nz - 1, (0,))
    xstep(nz - 1)
    ystep(nz - 1, far)

    for a in range(2):
        pltpu.make_async_copy(
            stage.at[a], out[a].at[pl.ds(pl.multiple_of(z * rows, rows), rows)], lsem.at[a]).wait()
    for dist in range(0, nz):
        for a in range(2):
            for right in (True, False):
                k = 0 if right else 1
                if dist < nz - 1:
                    cond = can[right] if dist == 0 else has(dist, right) & can[right]
                    when(cond, lambda a=a, right=right: zsend(a, dist, right).wait_send())
                if dist > 0:
                    def fin(a=a, right=right, k=k):
                        for d in range(1, nx):
                            xcopy(a, k, dist, d, right, True).wait_send()
                        for d in range(nx):
                            ccopy(a, k, dist, d, right, True).wait_send()
                            ccopy(a, k, dist, d, right, False).wait_recv()
                            if a == 1 and split:
                                ycopy(k, dist, d, right, True).wait_send()
                                fcopy(k, dist, d, right, True).wait_send()
                                fcopy(k, dist, d, right, False).wait_recv()
                    when(has(dist, right), fin)


def gather_inputs(nuc, loc, nz, nm):
    rows, width = nuc.shape
    nx = nm // 2
    dma = pltpu.SemaphoreType.DMA
    anyspec = pl.BlockSpec(memory_space=pl.ANY)
    shape = jax.ShapeDtypeStruct((nz * rows, width), bf16)
    ex = (2, nz - 1, nx) if halves(rows, nm) else (1,)
    return pl.pallas_call(
        functools.partial(gather_kernel, nz, nm),
        out_shape=(shape, shape),
        in_specs=[anyspec] * 2,
        out_specs=[anyspec] * 2,
        scratch_shapes=[
            pltpu.VMEM((2, rows, width), bf16),
            dma((2,)),
            dma((2, 2, nz)), dma((2, 2, nz)),
            dma((2, 2, nz - 1, nx)), dma((2, 2, nz - 1, nx)),
            dma((2, 2, nz - 1, nx)), dma((2, 2, nz - 1, nx)),
            dma(ex), dma(ex), dma(ex), dma(ex),
        ],
        compiler_params=pltpu.CompilerParams(collective_id=0, has_side_effects=True),
        name="gather_inputs",
    )(nuc, loc)


def attend_kernel(nz, nm, heads, qk, vd, sharp, nuc, loc, gain, wqk, wv, mix, out, mix_all,
                  q_s, k_s, v_s, xs, xr, ys, yr, cs, cr, os, orr):
    share_mix(nz, nm, mix, mix_all, xs, xr, ys, yr, cs, cr, os, orr, 0)
    t, j = pl.program_id(0), pl.program_id(1)
    z = lax.axis_index("seq")
    rows = nuc.shape[0]
    b = 128

    def body(flip):
        r_i = lax.broadcasted_iota(jnp.int32, (b, b), 0)
        c_i = lax.broadcasted_iota(jnp.int32, (b, b), 1)
        anti = jnp.where(r_i + c_i == b - 1, 1.0, 0.0).astype(bf16)
        parts = []
        nb = rows // b
        for i in range(nb):
            if flip:
                l = jnp.dot(anti, loc[(nb - 1 - i) * b:(nb - i) * b, :], preferred_element_type=f32)
            else:
                l = loc[i * b:(i + 1) * b, :].astype(f32)
            s = nuc[i * b:(i + 1) * b, :].astype(f32) + l
            parts.append((normalize(s) * gain[...]).astype(bf16))
        normed = jnp.concatenate(parts, axis=0)
        here = pl.ds(pl.multiple_of(j * rows, rows), rows)
        key = jnp.dot(normed, wqk[1], preferred_element_type=f32)
        for h in range(heads):
            k_s[here, h * qk:(h + 1) * qk] = normalize(key[:, h * qk:(h + 1) * qk]).astype(bf16)
        v_s[here, :] = jnp.dot(normed, wv[...], preferred_element_type=f32).astype(bf16)

        @pl.when(j == z)
        def _():
            query = jnp.dot(normed, wqk[0], preferred_element_type=f32)
            for h in range(heads):
                q_s[:, h * qk:(h + 1) * qk] = normalize(query[:, h * qk:(h + 1) * qk]).astype(bf16)

    @pl.when(t == 0)
    def _():
        body(False)

    @pl.when(t == 1)
    def _():
        body(True)

    @pl.when(j == nz - 1)
    def _():
        s_all = k_s.shape[0]
        chunk = 128
        wide = heads * vd
        for i in range(rows // chunk):
            rr = slice(i * chunk, (i + 1) * chunk)
            if i == 1:
                share_mix(nz, nm, mix, mix_all, xs, xr, ys, yr, cs, cr, os, orr, 2)
            res = []
            for h in range(heads):
                lo = (h * vd) // 128 * 128
                hi = min(-(-((h + 1) * vd) // 128) * 128, wide)
                num = jnp.zeros((chunk, hi - lo), f32)
                tot = jnp.zeros((chunk, 1), f32)
                step = 1536
                for kk in range(0, s_all, step):
                    sc = lax.dot_general(
                        q_s[rr, h * qk:(h + 1) * qk], k_s[kk:kk + step, h * qk:(h + 1) * qk],
                        (((1,), (1,)), ((), ())), preferred_element_type=f32)
                    w = jnp.exp(sc * (sharp[h] / qk))
                    tot = tot + jnp.sum(w, axis=-1, keepdims=True)
                    num = num + jnp.dot(w.astype(bf16), v_s[kk:kk + step, lo:hi],
                                        preferred_element_type=f32)
                res.append((lo, hi, num / tot))
            if heads == 1:
                out[rr, :] = res[0][2].astype(bf16)
            else:
                for lo in range(0, wide, 128):
                    hi = min(lo + 128, wide)
                    col = lo + lax.broadcasted_iota(jnp.int32, (chunk, hi - lo), 1)
                    val = None
                    for h in range(heads):
                        l0, h0, r = res[h]
                        if h * vd < hi and (h + 1) * vd > lo:
                            v = r[:, lo - l0:hi - l0]
                            val = v if val is None else jnp.where(col < h * vd, val, v)
                    out[rr, lo:hi] = val.astype(bf16)

    share_mix(nz, nm, mix, mix_all, xs, xr, ys, yr, cs, cr, os, orr, 1)


def share_mix(nz, nm, mix, mix_all, xs, xr, ys, yr, cs, cr, os, orr, phase):
    nx = nm // 2
    step = pl.program_id(0) * nz + pl.program_id(1)
    m = lax.axis_index("mp")
    g = lax.axis_index("groups")
    x, c = m // 2, m % 2
    n = 4 if mix.shape[0] % 128 == 0 else 2
    size = mix.shape[0] // (2 * n)

    def rows(gg, p):
        return pl.ds(pl.multiple_of((gg * n + p) * size, size), size)

    def xcopy(p, d, mine):
        o = lax.rem(x + d, nx) if mine else lax.rem(x - d + nx, nx)
        k = m if mine else o * 2 + c
        return pltpu.make_async_remote_copy(
            src_ref=mix.at[rows(g, p)], dst_ref=mix_all.at[k, rows(g, p)],
            send_sem=xs.at[p, d - 1], recv_sem=xr.at[p, d - 1],
            device_id={"mp": o * 2 + c}, device_id_type=MESH)

    def ycopy(p, d, mine):
        k = lax.rem(x - d + nx, nx) * 2 + c
        r = rows(g if mine else 1 - g, p)
        return pltpu.make_async_remote_copy(
            src_ref=mix_all.at[k, r], dst_ref=mix_all.at[k, r],
            send_sem=ys.at[p, d - 1], recv_sem=yr.at[p, d - 1],
            device_id={"groups": 1 - g}, device_id_type=MESH)

    def ccopy(p, d, far, mine):
        k = lax.rem(x - d + nx, nx) * 2 + (c if mine else 1 - c)
        r = rows(1 - g if far else g, p)
        f = 1 if far else 0
        return pltpu.make_async_remote_copy(
            src_ref=mix_all.at[k, r], dst_ref=mix_all.at[k, r],
            send_sem=cs.at[p, d - 1, f], recv_sem=cr.at[p, d - 1, f],
            device_id={"mp": x * 2 + 1 - c}, device_id_type=MESH)

    def own(mine):
        return pltpu.make_async_remote_copy(
            src_ref=mix, dst_ref=mix_all.at[m if mine else x * 2 + 1 - c],
            send_sem=os, recv_sem=orr,
            device_id={"mp": x * 2 + 1 - c}, device_id_type=MESH)

    def pass_on(p):
        for d in range(1, nx):
            xcopy(p, d, False).wait_recv()
            ycopy(p, d, True).start()
            ccopy(p, d, False, True).start()

    def bring(p):
        for d in range(1, nx):
            ycopy(p, d, False).wait_recv()
            ccopy(p, d, True, True).start()

    if phase == 0:
        @pl.when(step == 0)
        def _():
            barrier = pltpu.get_barrier_semaphore()
            for d in range(1, nx):
                pl.semaphore_signal(barrier, inc=1, device_id={"mp": lax.rem(x + d, nx) * 2 + c}, device_id_type=MESH)
            pl.semaphore_signal(barrier, inc=1, device_id={"mp": x * 2 + 1 - c}, device_id_type=MESH)
            pl.semaphore_signal(barrier, inc=1, device_id={"groups": 1 - g}, device_id_type=MESH)
            pl.semaphore_wait(barrier, nx + 1)
            for p in range(n):
                for d in range(1, nx):
                    xcopy(p, d, True).start()
            own(True).start()

        turns = {4: (nz - 1, None, nz, nz + 2), 2: (nz, nz + 2)}[n]
        for p in range(n):
            if turns[p] is not None:
                pl.when(step == turns[p])(functools.partial(pass_on, p))

        @pl.when(step == 2 * nz - 1)
        def _():
            for p in range(n // 2):
                bring(p)
    elif phase == 2:
        if n == 4:
            pl.when(step == nz - 1)(functools.partial(pass_on, 1))
    else:
        @pl.when(step == 2 * nz - 1)
        def _():
            for p in range(n // 2, n):
                bring(p)
            own(True).wait_send()
            own(False).wait_recv()
            for p in range(n):
                for d in range(1, nx):
                    xcopy(p, d, True).wait_send()
                    ycopy(p, d, True).wait_send()
                    for far in (False, True):
                        ccopy(p, d, far, True).wait_send()
                        ccopy(p, d, far, False).wait_recv()


def attend(nuc_all, loc_all, gain, wqk, wv, sharp, mix, nz, nm, rows):
    heads = sharp.shape[0]
    width = nuc_all.shape[1]
    qk = wqk.shape[2] // heads
    vd = wv.shape[1] // heads
    s_all = nuc_all.shape[0]
    nx = nm // 2
    dma = pltpu.SemaphoreType.DMA
    full = lambda a: pl.BlockSpec(a.shape, lambda t, j: (0,) * a.ndim, pipeline_mode=pl.Buffered(1))
    anyspec = pl.BlockSpec(memory_space=pl.ANY)
    gain = gain.reshape(1, width)
    return pl.pallas_call(
        functools.partial(attend_kernel, nz, nm, heads, qk, vd),
        grid=(2, nz),
        out_shape=(jax.ShapeDtypeStruct((2, rows, heads * vd), bf16),
                   jax.ShapeDtypeStruct((nm,) + mix.shape, bf16)),
        in_specs=[
            pl.BlockSpec(memory_space=pltpu.SMEM),
            pl.BlockSpec((rows, width), lambda t, j: (j, 0)),
            pl.BlockSpec((rows, width), lambda t, j: (t * (nz - 1 - j) + (1 - t) * j, 0)),
            full(gain), full(wqk), full(wv), anyspec,
        ],
        out_specs=(pl.BlockSpec((pl.Squeezed(), rows, heads * vd), lambda t, j: (t, 0, 0)), anyspec),
        scratch_shapes=[
            pltpu.VMEM((rows, heads * qk), bf16),
            pltpu.VMEM((s_all, heads * qk), bf16),
            pltpu.VMEM((s_all, heads * vd), bf16),
            dma((4, nx)), dma((4, nx)), dma((4, nx)), dma((4, nx)),
            dma((4, nx, 2)), dma((4, nx, 2)), dma, dma,
        ],
        compiler_params=pltpu.CompilerParams(
            collective_id=2, has_side_effects=True, vmem_limit_bytes=56 << 20),
        name="attend",
    )(sharp, nuc_all, loc_all, gain, wqk, wv, mix)


def tail_kernel(nz, nm, att, nuc_h, loc_h, loc_all, gain, mix, mix_all, widen_h, narrow_h, out,
                att_all, nuc, loc, locm, mixv, widen, narrow, sbuf, rbuf, mid,
                lsem, msem, xs, xr, cs, cr, ss, sr):
    nx = nm // 2
    rows, width = nuc.shape
    share = width // nm
    b = 128
    parts = rows // b
    z = lax.axis_index("seq")
    m = lax.axis_index("mp")
    x, c = m // 2, m % 2
    barrier = pltpu.get_barrier_semaphore()
    for d in range(1, nm):
        pl.semaphore_signal(barrier, inc=1, device_id={"mp": lax.rem(m + d, nm)}, device_id_type=MESH)
    loads = [
        pltpu.make_async_copy(att, att_all.at[m], lsem.at[0]),
        pltpu.make_async_copy(nuc_h, nuc, lsem.at[1]),
        pltpu.make_async_copy(loc_h, loc, lsem.at[2]),
        pltpu.make_async_copy(loc_all.at[pl.ds(pl.multiple_of((nz - 1 - z) * rows, rows), rows)], locm, lsem.at[3]),
        pltpu.make_async_copy(widen_h, widen, lsem.at[4]),
        pltpu.make_async_copy(narrow_h, narrow, lsem.at[5]),
    ]
    mloads = [pltpu.make_async_copy(mix, mixv.at[m], msem.at[0])]
    for d in range(1, nm):
        k = lax.rem(m + d, nm)
        mloads.append(pltpu.make_async_copy(mix_all.at[k], mixv.at[k], msem.at[d]))
    for cp in loads[:4] + mloads + loads[4:]:
        cp.start()
    pl.semaphore_wait(barrier, nm - 1)

    def xcopy(i, d, mine):
        o = lax.rem(x + d, nx) if mine else lax.rem(x - d + nx, nx)
        k = m if mine else o * 2 + c
        r = pl.ds(i * b, b)
        return pltpu.make_async_remote_copy(
            src_ref=att.at[:, r], dst_ref=att_all.at[k, :, r], send_sem=xs.at[i, d - 1],
            recv_sem=xr.at[i, d - 1], device_id={"mp": o * 2 + c}, device_id_type=MESH)

    def ccopy(i, d, mine):
        o = lax.rem(x - d + nx, nx)
        k = o * 2 + (c if mine else 1 - c)
        r = pl.ds(i * b, b)
        ref = att.at[:, r] if d == 0 else att_all.at[k, :, r]
        return pltpu.make_async_remote_copy(
            src_ref=ref, dst_ref=att_all.at[k, :, r], send_sem=cs.at[i, d], recv_sem=cr.at[i, d],
            device_id={"mp": x * 2 + 1 - c}, device_id_type=MESH)

    def scopy(i, d):
        k = lax.rem(m + d, nm)
        return pltpu.make_async_remote_copy(
            src_ref=sbuf.at[i, k], dst_ref=rbuf.at[i, d - 1], send_sem=ss.at[i, d - 1],
            recv_sem=sr.at[i, d - 1], device_id={"mp": k}, device_id_type=MESH)

    for i in range(parts):
        for d in range(1, nx):
            xcopy(i, d, True).start()
        ccopy(i, 0, True).start()

    def pass_on(i):
        for d in range(1, nx):
            xcopy(i, d, False).wait_recv()
            ccopy(i, d, True).start()

    r_i = lax.broadcasted_iota(jnp.int32, (b, b), 0)
    c_i = lax.broadcasted_iota(jnp.int32, (b, b), 1)
    anti = jnp.where(r_i + c_i == b - 1, 1.0, 0.0).astype(bf16)
    for cp in loads[:4]:
        cp.wait()
    pass_on(0)
    for cp in mloads:
        cp.wait()
    for i in range(parts):
        r = slice(i * b, (i + 1) * b)
        n = nuc[r, :].astype(f32)
        s0 = n + loc[r, :].astype(f32)
        s1 = n + jnp.dot(anti, locm[(parts - 1 - i) * b:(parts - i) * b, :], preferred_element_type=f32)
        middle = jnp.concatenate([s0, s1], axis=0)
        for d in range(nx):
            ccopy(i, d, False).wait_recv()
        for k in range(nm):
            a = jnp.concatenate([att_all[k, 0, r, :], att_all[k, 1, r, :]], axis=0)
            middle = middle + jnp.dot(a, mixv[k], preferred_element_type=f32)
        if i + 1 < parts:
            pass_on(i + 1)
        normed = (normalize(middle) * gain[...]).astype(bf16)
        if i == 0:
            for cp in loads[4:]:
                cp.wait()
        up = jax.nn.gelu(jnp.dot(normed, widen[...], preferred_element_type=f32), approximate=True)
        both = (up[:b] + up[b:]).astype(bf16)
        down = jnp.dot(both, narrow[...], preferred_element_type=f32)
        total = middle[:b] + middle[b:] + down
        down = down.astype(bf16)
        for k in range(nm):
            sbuf[i, k] = down[:, k * share:(k + 1) * share]
            mid[i, k] = total[:, k * share:(k + 1) * share]
        for d in range(1, nm):
            scopy(i, d).start()
    for i in range(parts):
        acc = mid[i, m]
        for d in range(1, nm):
            scopy(i, d).wait_recv()
            acc = acc + rbuf[i, d - 1].astype(f32)
        out[i * b:(i + 1) * b, :] = 0.5 * acc
    for i in range(parts):
        for d in range(1, nx):
            xcopy(i, d, True).wait_send()
        for d in range(nx):
            ccopy(i, d, True).wait_send()
        for d in range(1, nm):
            scopy(i, d).wait_send()


def tail(att, nuc, loc, loc_all, gain, mix, mix_all, widen, narrow, nz, nm):
    rows, width = nuc.shape
    share = width // nm
    nx = nm // 2
    parts = rows // 128
    dma = pltpu.SemaphoreType.DMA
    anyspec = pl.BlockSpec(memory_space=pl.ANY)
    vm = pl.BlockSpec(memory_space=pltpu.VMEM)
    v = pltpu.VMEM
    return pl.pallas_call(
        functools.partial(tail_kernel, nz, nm),
        out_shape=jax.ShapeDtypeStruct((rows, share), f32),
        in_specs=[vm, anyspec, anyspec, anyspec, vm, anyspec, anyspec, anyspec, anyspec],
        out_specs=vm,
        scratch_shapes=[
            v((nm,) + att.shape, bf16), v(nuc.shape, bf16), v(nuc.shape, bf16), v(nuc.shape, bf16),
            v((nm,) + mix.shape, bf16), v(widen.shape, bf16), v(narrow.shape, bf16),
            v((parts, nm, 128, share), bf16), v((parts, nm - 1, 128, share), bf16),
            v((parts, nm, 128, share), f32),
            dma((6,)), dma((nm,)),
            dma((parts, nx)), dma((parts, nx)), dma((parts, nx)), dma((parts, nx)),
            dma((parts, nm)), dma((parts, nm)),
        ],
        compiler_params=pltpu.CompilerParams(
            collective_id=3, has_side_effects=True, vmem_limit_bytes=56 << 20),
        name="tail",
    )(att, nuc, loc, loc_all, gain.reshape(1, width), mix, mix_all, widen, narrow)


def shards(nuc, loc, premix, wqk, wv, sharp, mixing, premlp, widen, narrow):
    rows = nuc.shape[0]
    nz, nm = lax.axis_size("seq"), lax.axis_size("mp")
    nuc_all, loc_all = gather_inputs(nuc, loc, nz, nm)
    att, mix_all = attend(nuc_all, loc_all, premix, wqk, wv, sharp, mixing, nz, nm, rows)
    return tail(att, nuc, loc, loc_all, premlp, mixing, mix_all, widen, narrow, nz, nm)


def solution(mesh):
    return jax.shard_map(
        shards,
        mesh=mesh,
        in_specs=(
            P(("groups", "seq"), None),
            P("seq", None),
            P(),
            P(None, None, "mp"),
            P(None, "mp"),
            P("mp"),
            P("mp", None),
            P(),
            P(None, "mp"),
            P("mp", None),
        ),
        out_specs=P(("groups", "seq"), "mp"),
        check_vma=False,
    )
```
